256 devices in a mesh: wide: 64 (over x, y_lo, z), narrow: 4 (over y_hi, core).
Axes of the slice: x: 4, y: 4 (y_hi: 2, y_lo: 2; y = y_hi * 2 + y_lo), z: 8, core: 2. Of those that a mesh axis runs over, the one named last changes fastest.
Arguments:
- queries: bfloat16 [32768, 512], P(('wide', 'narrow')), may hold values from -160 to 160, as said below
- keys: bfloat16 [32768, 512], P(('wide', 'narrow')), may hold values from -4 to 4
- values: bfloat16 [32768, 512], P(('wide', 'narrow')), may hold values from -6 to 6
- side_keys: bfloat16 [32768, 512], P(('wide', 'narrow')), may hold values from -4 to 4
- side_values: bfloat16 [32768, 512], P(('wide', 'narrow')), may hold values from -6 to 6
- positions: int32 [32768], P(('wide', 'narrow')), may hold values from 0 to 2047, as said below
- gain: float32 [512], replicated, may hold values from 0.5 to 1.5
Outputs:
- mixed: bfloat16 [32768, 512], P(('wide', 'narrow'))
The draws below stay inside these ranges and needn't reach their ends.
Inputs may be any that keep to these rules, and one draw needn't show every extreme that they name: `queries`: queries of order one; some rows may be many times larger. Documents are contiguous runs of tokens; positions count from 0 at a document's first token and rise by one along it; token 0 has position 0; a document holds at most 2048 tokens; tokens 0 to 1023 form one document and a new document begins at every token whose index leaves the remainder 2048 / 2 when divided by 2048.
All inputs are finite; a program needn't handle non-finite values.
Results may differ from the reference program's by a relative error of at most 0.0077.
Values may be sent and summed in bfloat16 or wider, within the bound.
No kernel may reach another device: no remote copies, remote signals or barrier semaphores. Data moves between devices by JAX's collectives and lax.ppermute only.
A program may use at most 64 MiB of HBM per device.

```python
import jax
import jax.numpy as jnp
from jax import lax

HEADS = 4
HEAD_DIM = 128
W1 = 512
W2 = 32
DOC_MAX = 2048
SEQ = 32768


def draw_queries(key, part):
    base = jnp.clip(jax.random.normal(key, (SEQ, HEADS * HEAD_DIM), jnp.float32), -4.0, 4.0)
    return base.astype(jnp.bfloat16)


def draw_positions(key, part):
    index = jnp.arange(SEQ, dtype=jnp.int32)
    remain = index % DOC_MAX
    half = DOC_MAX // 2
    regular = (index == 0) | (remain == half)
    extra = jax.random.randint(jax.random.fold_in(key, 3), (SEQ,), 0, 16) == 0
    extra = extra & (index >= DOC_MAX) & (remain > half) & (remain < DOC_MAX - W1)
    boundary = regular | extra
    starts = lax.cummax(jnp.where(boundary, index, 0), axis=0)
    return (index - starts).astype(jnp.int32)


def level_of(rng, shape, cuts, smallest, high):
    loudness = 1.0
    for axis_at, blocks in cuts:
        heights = jax.random.uniform(jax.random.fold_in(jax.random.fold_in(rng, 6), axis_at), (blocks,), jnp.float32, smallest / len(cuts), high / len(cuts))
        loudness = loudness * jnp.repeat(jnp.exp(heights), shape[axis_at] // blocks).reshape((-1,) + (1,) * (len(shape) - 1 - axis_at))
    return loudness


def normal_values(own_key, dims, deviation, most, cuts=(), held_as=jnp.bfloat16):
    level = level_of(own_key, dims, cuts, -0.22, 0.18) if cuts else 1.0
    values = jax.random.normal(own_key, dims, jnp.float32) * deviation * level
    return jnp.minimum(jnp.maximum(values, -most), most).astype(held_as)


def setup_inputs(seed: int = 0) -> dict:
    arg_keys = jax.random.split(jax.random.key(seed), 8)
    queries = draw_queries(jax.random.fold_in(arg_keys[7], 71), 0)
    keys = normal_values(arg_keys[1], (SEQ, HEADS * HEAD_DIM), 1.0, 4.0, ((0, 256),))
    values = normal_values(arg_keys[2], (SEQ, HEADS * HEAD_DIM), 1.0, 6.0, ((0, 256),))
    side_keys = normal_values(arg_keys[3], (SEQ, HEADS * HEAD_DIM), 1.0, 4.0, ((0, 256),))
    side_values = normal_values(arg_keys[4], (SEQ, HEADS * HEAD_DIM), 1.0, 6.0, ((0, 256),))
    positions = draw_positions(jax.random.fold_in(arg_keys[7], 71), 0)
    gain = jnp.clip(1.0 + 0.1 * jax.random.normal(arg_keys[6], (HEADS * HEAD_DIM,), jnp.float32), 0.5, 1.5)
    return dict(queries=queries, keys=keys, values=values, side_keys=side_keys, side_values=side_values, positions=positions, gain=gain)


query_rows = 32

def window_block(query_blk, side_key_stack, side_value_stack, key_win, value_win, pos_blk, gain):
    span = key_win.shape[0]
    local = jnp.arange(query_rows, dtype=jnp.int32)
    column = jnp.arange(span, dtype=jnp.int32)
    dist = W1 + local[:, None] - column[None, :]
    valid_key = (dist >= 0) & (dist < W1) & (dist <= pos_blk[:, None])
    offset = jnp.arange(W2, dtype=jnp.int32)
    valid_side = offset[None, :] <= pos_blk[:, None]
    allowed = valid_side[:, :, None] & valid_key[:, None, :]
    scale = 1.0 / HEAD_DIM ** 0.5
    pieces = []
    for head in range(HEADS):
        lo = head * HEAD_DIM
        hi = lo + HEAD_DIM
        q_head = query_blk[:, lo:hi].astype(jnp.float32)
        pair = (q_head[:, None, :] * side_key_stack[:, :, lo:hi].astype(jnp.float32)).astype(jnp.bfloat16)
        pair = pair.reshape(query_rows * W2, HEAD_DIM)
        score = lax.dot_general(pair, key_win[:, lo:hi], (((1,), (1,)), ((), ())), preferred_element_type=jnp.float32)
        score = score.reshape(query_rows, W2, span) * scale
        score = jnp.where(allowed, score, -jnp.inf)
        top = lax.optimization_barrier(jnp.max(score, axis=(1, 2), keepdims=True))
        weight = jnp.exp(score - top)
        total = lax.optimization_barrier(jnp.sum(weight, axis=(1, 2)))
        weight_b = weight.astype(jnp.bfloat16).reshape(query_rows * W2, span)
        inner = jnp.dot(weight_b, value_win[:, lo:hi], preferred_element_type=jnp.float32)
        inner = inner.reshape(query_rows, W2, HEAD_DIM)
        attended = lax.optimization_barrier(jnp.sum(inner * side_value_stack[:, :, lo:hi].astype(jnp.float32), axis=1)) / total[:, None]
        normed = attended * lax.rsqrt(lax.optimization_barrier(jnp.mean(attended * attended, axis=-1, keepdims=True)) + 1e-06)
        pieces.append(normed * gain[lo:hi].astype(jnp.float32))
    return jnp.concatenate(pieces, axis=-1).astype(jnp.bfloat16)

def side_stack(ext_side, start):
    rows_list = [lax.dynamic_slice_in_dim(ext_side, start + W2 - offset, query_rows, 0) for offset in range(W2)]
    return jnp.stack(rows_list, axis=1)

def reference(queries, keys, values, side_keys, side_values, positions, gain):
    width = HEADS * HEAD_DIM
    key_pad = jnp.concatenate([jnp.zeros((W1, width), keys.dtype), keys], axis=0)
    value_pad = jnp.concatenate([jnp.zeros((W1, width), values.dtype), values], axis=0)
    side_key_pad = jnp.concatenate([jnp.zeros((W2, width), side_keys.dtype), side_keys], axis=0)
    side_value_pad = jnp.concatenate([jnp.zeros((W2, width), side_values.dtype), side_values], axis=0)

    def one_block(index):
        start = (index * query_rows).astype(jnp.int32)
        query_blk = lax.dynamic_slice_in_dim(queries, start, query_rows, 0)
        pos_blk = lax.dynamic_slice_in_dim(positions, start, query_rows, 0)
        key_win = lax.dynamic_slice_in_dim(key_pad, start, W1 + query_rows, 0)
        value_win = lax.dynamic_slice_in_dim(value_pad, start, W1 + query_rows, 0)
        return window_block(query_blk, side_stack(side_key_pad, start), side_stack(side_value_pad, start), key_win, value_win, pos_blk, gain)
    blocks = lax.map(one_block, jnp.arange(SEQ // query_rows, dtype=jnp.int32))
    return blocks.reshape(SEQ, width)
```

```python
import functools

import jax
import jax.numpy as jnp
from jax import lax
from jax.experimental import pallas as pl
from jax.experimental.pallas import tpu as pltpu
from jax.sharding import PartitionSpec as P

HEADS = 4
HEAD_DIM = 128
W1 = 512
W2 = 32
ROWS = 128
SUB = 32
NSUB = ROWS // SUB
LANES = W2 * SUB
PACK = 2 * ROWS + 2 * W2
SCALE_LOG2E = 1.4426950408889634 / HEAD_DIM**0.5
MASKED = -1e30
AXES = ("wide", "narrow")


f32 = jnp.float32
bf16 = jnp.bfloat16


def iota(shape, axis):
    return lax.broadcasted_iota(jnp.int32, shape, axis)


def key_bias(pos, base, sub):
    shape = (ROWS, 128)
    column = iota(shape, 1)
    dist = W1 + sub * SUB + column - base - iota(shape, 0)
    allowed = (dist >= 0) & (dist < W1) & (dist <= pos)
    bias = jnp.where(allowed, 0.0, MASKED)
    bias = jnp.where(column < SUB, bias, jnp.where(column == SUB, MASKED, 0.0))
    return bias.astype(bf16)


def sub_positions(pos, sub):
    return pos if sub == 0 else pltpu.roll(pos, 128 - sub * SUB, 1)


def fill_onehot(onehot_ref, pos, subs):
    pos_rows = jnp.transpose(jnp.broadcast_to(pos, (ROWS, 128)))
    column = iota((SUB, 128), 1)
    hot = jnp.where(column == iota((SUB, 128), 0), 1.0, 0.0)
    for sub in subs:
        rows = pos_rows[sub * SUB : (sub + 1) * SUB]
        for offset in range(W2):
            bad = (rows < offset) & (column == SUB)
            onehot_ref[sub, offset * SUB : (offset + 1) * SUB, :] = jnp.where(bad, 1.0, hot).astype(bf16)


def pair_rows(q, sk_ref, onehot_ref, head, sub):
    first = W2 + sub * SUB
    parts = [
        (q * sk_ref[head, pl.ds(first - offset, SUB), :]).astype(bf16) for offset in range(W2)
    ]
    return jnp.concatenate([jnp.concatenate(parts, axis=0), onehot_ref[sub]], axis=1)


def side_columns(sv_ref, head, sub):
    first = W2 + sub * SUB
    parts = [sv_ref[head, pl.ds(first - offset, SUB), :] for offset in range(W2)]
    return jnp.transpose(jnp.concatenate(parts, axis=0))


def fold(x, op):
    y = x[:, :128]
    for i in range(1, LANES // 128):
        y = op(y, x[:, i * 128 : (i + 1) * 128])
    y = op(y, pltpu.roll(y, 64, 1))
    return op(y, pltpu.roll(y, 32, 1))


def scores(keys, bias, rhs):
    lhs = jnp.concatenate([keys, bias], axis=1)
    return lax.dot_general(lhs, rhs, (((1,), (1,)), ((), ())), preferred_element_type=f32)


def load_sides(sk_ref, sv_ref, sk, sv, first):
    for head in range(HEADS):
        lo = head * HEAD_DIM
        rows = sk.shape[0]
        sk_ref[head, first : first + rows, :] = sk[:, lo : lo + HEAD_DIM].astype(f32)
        sv_ref[head, first : first + rows, :] = sv[:, lo : lo + HEAD_DIM].astype(f32)


def load_values(vt_ref, tile, values):
    for head in range(HEADS):
        lo = head * HEAD_DIM
        vt_ref[head, tile, :HEAD_DIM, :] = jnp.transpose(values[:, lo : lo + HEAD_DIM])
        vt_ref[head, tile, HEAD_DIM:, :] = jnp.ones((16, ROWS), bf16)


def row_range(kind, sub):
    if kind == "own":
        return 0, SUB * (sub + 1)
    if kind == "far":
        return SUB * sub, ROWS
    return 0, ROWS


def run_tiles(kinds, subs_of, keys_of, q_ref, sk_ref, sv_ref, onehot_ref, bias_ref, vt_ref, acc_ref, tot_ref, fresh):
    lane = iota((1, 128), 1) // SUB

    def one_head(head, carry):
        at = pl.multiple_of(head * HEAD_DIM, HEAD_DIM)
        acc = jnp.zeros((HEAD_DIM, 128), f32)
        tot = jnp.zeros((8, 128), f32)
        for sub in range(NSUB):
            tiles = [t for t in range(len(kinds)) if sub in subs_of[t]]
            if not tiles:
                continue
            q = q_ref[sub * SUB : (sub + 1) * SUB, pl.ds(at, HEAD_DIM)].astype(f32)
            rhs = pair_rows(q, sk_ref, onehot_ref, head, sub)
            weights, values = [], []
            for t in tiles:
                lo, hi = row_range(kinds[t], sub)
                score = scores(keys_of[t](at, lo, hi), bias_ref[t, sub, lo:hi, :], rhs)
                weight = jnp.exp2(score * SCALE_LOG2E).astype(bf16)
                if lo > 0:
                    weights.append(jnp.zeros((lo, LANES), bf16))
                weights.append(weight)
                if hi < ROWS:
                    weights.append(jnp.zeros((ROWS - hi, LANES), bf16))
                values.append(vt_ref[head, t])
            inner = jnp.dot(
                jnp.concatenate(values, axis=1),
                jnp.concatenate(weights, axis=0),
                preferred_element_type=f32,
            )
            part = fold(inner[:HEAD_DIM] * side_columns(sv_ref, head, sub), jnp.add)
            count = fold(inner[HEAD_DIM : HEAD_DIM + 8], jnp.add)
            acc = jnp.where(lane == sub, part, acc)
            tot = jnp.where(lane == sub, count, tot)
        if fresh:
            acc_ref[head] = acc
            tot_ref[head] = tot
        else:
            acc_ref[head] += acc
            tot_ref[head] += tot
        return carry

    lax.fori_loop(0, HEADS, one_head, 0)


def keys_at(ref):
    return lambda at, lo, hi: ref[lo:hi, pl.ds(at, HEAD_DIM)]


def near_kernel(kind, base, q_ref, k_ref, v_ref, sk_in, sv_in, pos_ref, acc_ref, tot_ref, sk_ref, sv_ref, onehot_ref, bias_ref, vt_ref):
    subs = (1, 2, 3)
    pos = pos_ref[...]
    fill_onehot(onehot_ref, pos, subs)
    for sub in subs:
        bias_ref[0, sub] = key_bias(sub_positions(pos, sub), base, sub)
    load_sides(sk_ref, sv_ref, sk_in[...], sv_in[...], W2)
    load_values(vt_ref, 0, v_ref[...])
    run_tiles([kind], [subs], [keys_at(k_ref)], q_ref, sk_ref, sv_ref, onehot_ref, bias_ref, vt_ref, acc_ref, tot_ref, True)


def mid_kernel(q_ref, k_ref, v_ref, sk_in, sv_in, pos_ref, acc_a, tot_a, acc_b, tot_b, near_ref, swap_ref, far_ref, rim_odd, rim_even, acc_ref, tot_ref, sk_ref, sv_ref, onehot_ref, bias_ref, vt_ref):
    odd = lax.rem(lax.axis_index("narrow"), 2)
    pos = pos_ref[...]
    every = (0, 1, 2, 3)
    fill_onehot(onehot_ref, pos, every)
    bases = (W1, W1 - 2 * ROWS, W1 - ROWS - 2 * ROWS * odd, 0)
    subs_of = ((0,), (0,), every, every)
    for t in range(4):
        for sub in subs_of[t]:
            bias_ref[t, sub] = key_bias(sub_positions(pos, sub), bases[t], sub)
    load_sides(sk_ref, sv_ref, sk_in[...], sv_in[...], W2)
    rim = jnp.where(odd == 1, rim_odd[...].astype(f32), rim_even[...].astype(f32))
    load_sides(sk_ref, sv_ref, rim[:W2], rim[W2:], 0)
    load_values(vt_ref, 0, v_ref[...])
    for t, ref in ((1, near_ref), (2, swap_ref), (3, far_ref)):
        load_values(vt_ref, t, ref[ROWS : 2 * ROWS, :])
    acc_ref[...] = acc_a[...] + acc_b[...]
    tot_ref[...] = tot_a[...] + tot_b[...]
    run_tiles(
        ["own", "full", "full", "far"], subs_of,
        [keys_at(k_ref), keys_at(near_ref), keys_at(swap_ref), keys_at(far_ref)],
        q_ref, sk_ref, sv_ref, onehot_ref, bias_ref, vt_ref, acc_ref, tot_ref, False,
    )


def last_kernel(q_ref, k_any, v_any, sk_in, sv_in, pos_ref, gain_ref, acc_in, tot_in, near_any, swap_any, far_any, odd_any, even_any, rim_odd, rim_even, out_ref, sk_ref, sv_ref, onehot_ref, bias_ref, vt_ref, acc_ref, tot_ref, last_ref, keys_ref, values_ref, sem):
    odd = lax.rem(lax.axis_index("narrow"), 2)
    even = odd == 0
    last = pltpu.make_async_copy(even_any, last_ref, sem)

    @pl.when(odd == 1)
    def _():
        copy = pltpu.make_async_copy(odd_any, last_ref, sem)
        copy.start()
        copy.wait()

    @pl.when(even)
    def _():
        last.start()
        last.wait()

    pos = pos_ref[...]
    every = (0, 1, 2, 3)
    fill_onehot(onehot_ref, pos, every)
    last_base = W1 - 3 * ROWS + 2 * ROWS * odd
    for sub in every:
        bias_ref[0, sub] = key_bias(sub_positions(pos, sub), last_base, sub)
    load_sides(sk_ref, sv_ref, sk_in[...], sv_in[...], W2)
    rim = jnp.where(odd == 1, rim_odd[...].astype(f32), rim_even[...].astype(f32))
    load_sides(sk_ref, sv_ref, rim[:W2], rim[W2:], 0)
    load_values(vt_ref, 0, last_ref[ROWS : 2 * ROWS, :])
    acc_ref[...] = acc_in[...]
    tot_ref[...] = tot_in[...]
    run_tiles(["full"], [every], [keys_at(last_ref)], q_ref, sk_ref, sv_ref, onehot_ref, bias_ref, vt_ref, acc_ref, tot_ref, False)

    total = tot_ref[...]
    good = jnp.where((total > 1e-18) & (total < 1e30), 1.0, 0.0)
    sound = jnp.min(good) > 0.5

    @pl.when(jnp.logical_not(sound))
    def _():
        copies = [(k_any, keys_ref.at[0]), (v_any, values_ref.at[0])]
        for t, ref in ((1, near_any), (2, swap_any), (3, far_any)):
            copies.append((ref.at[pl.ds(0, ROWS)], keys_ref.at[t]))
            copies.append((ref.at[pl.ds(ROWS, ROWS)], values_ref.at[t]))
        for source, target in copies:
            copy = pltpu.make_async_copy(source, target, sem)
            copy.start()
            copy.wait()
        keys_ref[4] = last_ref[:ROWS]
        values_ref[4] = last_ref[ROWS : 2 * ROWS]
        bases = (W1, W1 - 2 * ROWS, W1 - ROWS - 2 * ROWS * odd, 0, last_base)
        for t in range(5):
            load_values(vt_ref, t, values_ref[t])
            for sub in every:
                bias_ref[t, sub] = key_bias(sub_positions(pos, sub), bases[t], sub)
        lane = iota((1, 128), 1) // SUB

        def one(step, carry):
            head, sub = step // NSUB, lax.rem(step, NSUB)
            at = pl.multiple_of(head * HEAD_DIM, HEAD_DIM)
            q = q_ref[pl.ds(pl.multiple_of(sub * SUB, SUB), SUB), pl.ds(at, HEAD_DIM)].astype(f32)
            rhs = pair_rows(q, sk_ref, onehot_ref, head, sub)

            def tile_scores(t):
                return scores(keys_ref[t, :, pl.ds(at, HEAD_DIM)], bias_ref[t, sub], rhs) * SCALE_LOG2E

            def tile_top(t, top):
                return jnp.maximum(top, jnp.max(tile_scores(t), axis=0, keepdims=True))

            top = lax.fori_loop(0, 5, tile_top, jnp.full((1, LANES), -jnp.inf, f32))
            top = fold(jnp.broadcast_to(top, (8, LANES)), jnp.maximum)[:1]
            top = jnp.concatenate([top] * (LANES // 128), axis=1)

            def tile_inner(t, inner):
                weight = jnp.exp2(tile_scores(t) - top).astype(bf16)
                return inner + jnp.dot(vt_ref[head, t], weight, preferred_element_type=f32)

            inner = lax.fori_loop(0, 5, tile_inner, jnp.zeros((HEAD_DIM + 16, LANES), f32))
            part = fold(inner[:HEAD_DIM] * side_columns(sv_ref, head, sub), jnp.add)
            count = fold(inner[HEAD_DIM : HEAD_DIM + 8], jnp.add)
            acc_ref[head] = jnp.where(lane == sub, part, acc_ref[head])
            tot_ref[head] = jnp.where(lane == sub, count, tot_ref[head])
            return carry

        lax.fori_loop(0, HEADS * NSUB, one, 0)

    for head in range(HEADS):
        lo = head * HEAD_DIM
        attended = acc_ref[head] / tot_ref[head, :1]
        square = jnp.mean(attended * attended, axis=0, keepdims=True)
        normed = jnp.transpose(attended * lax.rsqrt(square + 1e-6))
        out_ref[:, lo : lo + HEAD_DIM] = (normed * gain_ref[:, lo : lo + HEAD_DIM]).astype(bf16)


def call(kernel, out_shape, in_spaces, tiles, extra, flops, name):
    vmem = pl.BlockSpec(memory_space=pltpu.VMEM)
    anywhere = pl.BlockSpec(memory_space=pl.ANY)
    side = pltpu.VMEM((HEADS, W2 + ROWS, HEAD_DIM), f32)
    return pl.pallas_call(
        kernel,
        out_shape=out_shape,
        in_specs=[anywhere if s else vmem for s in in_spaces],
        out_specs=jax.tree.map(lambda _: vmem, out_shape),
        scratch_shapes=[
            side,
            side,
            pltpu.VMEM((NSUB, LANES, 128), bf16),
            pltpu.VMEM((tiles, NSUB, ROWS, 128), bf16),
            pltpu.VMEM((HEADS, tiles, HEAD_DIM + 16, ROWS), bf16),
            *extra,
        ],
        compiler_params=pltpu.CompilerParams(vmem_limit_bytes=48 << 20),
        cost_estimate=pl.CostEstimate(flops=flops, bytes_accessed=1 << 20, transcendentals=0),
        name=name,
    )


PARTIAL = (
    jax.ShapeDtypeStruct((HEADS, HEAD_DIM, 128), f32),
    jax.ShapeDtypeStruct((HEADS, 8, 128), f32),
)
TILE_FLOPS = 4 * HEADS * ROWS * W2 * ROWS * HEAD_DIM


def body(queries, keys, values, side_keys, side_values, positions, gain):
    count = lax.axis_size(AXES)
    pos = positions.reshape(1, ROWS)
    gain = gain.reshape(1, HEADS * HEAD_DIM)
    packed = jnp.concatenate([keys, values, side_keys[ROWS - W2 :], side_values[ROWS - W2 :]], axis=0)
    swap = [(i, i ^ 1) for i in range(count)]

    def shift(by):
        return [(i, i + by) for i in range(count - by)]

    near = lax.ppermute(packed, AXES, shift(2))
    far = lax.ppermute(packed, AXES, shift(4))
    mate = lax.ppermute(packed, AXES, swap)
    near_mate = lax.ppermute(near, AXES, swap)
    far_mate = lax.ppermute(far, AXES, swap)

    sides = (side_keys, side_values, pos)
    acc_a, tot_a = call(
        functools.partial(near_kernel, "own", W1), PARTIAL, [0] * 6, 1, [], TILE_FLOPS, "own_tile"
    )(queries, keys, values, *sides)
    acc_b, tot_b = call(
        functools.partial(near_kernel, "full", W1 - 2 * ROWS), PARTIAL, [0] * 6, 1, [], TILE_FLOPS, "near_tile"
    )(queries, near[:ROWS], near[ROWS : 2 * ROWS], *sides)
    rim_odd, rim_even = mate[2 * ROWS :], near_mate[2 * ROWS :]
    acc_c, tot_c = call(mid_kernel, PARTIAL, [0] * 15, 4, [], 2 * TILE_FLOPS, "mid_tiles")(
        queries, keys, values, *sides, acc_a, tot_a, acc_b, tot_b, near, near_mate, far, rim_odd, rim_even
    )
    return call(
        last_kernel,
        jax.ShapeDtypeStruct((ROWS, HEADS * HEAD_DIM), bf16),
        [0, 1, 1, 0, 0, 0, 0, 0, 0, 1, 1, 1, 1, 1, 0, 0],
        5,
        [
            pltpu.VMEM((HEADS, HEAD_DIM, 128), f32),
            pltpu.VMEM((HEADS, 8, 128), f32),
            pltpu.VMEM((PACK, HEADS * HEAD_DIM), bf16),
            pltpu.VMEM((5, ROWS, HEADS * HEAD_DIM), bf16),
            pltpu.VMEM((5, ROWS, HEADS * HEAD_DIM), bf16),
            pltpu.SemaphoreType.DMA,
        ],
        TILE_FLOPS,
        "last_tile",
    )(queries, keys, values, *sides, gain, acc_c, tot_c, near, near_mate, far, mate, far_mate, rim_odd, rim_even)


def solution(mesh):
    split = P(AXES, None)
    return jax.shard_map(
        body,
        mesh=mesh,
        in_specs=(split, split, split, split, split, P(AXES), P()),
        out_specs=split,
        check_vma=False,
    )
```
